32 devices in a mesh: inter: 2 (over y), intra: 4 (over z), head: 4 (over x, core).
Axes of the slice: x: 2, y: 2, z: 4, core: 2. Of those that a mesh axis runs over, the one named last changes fastest.
Arguments:
- queries: bfloat16 [32, 1024, 128], P('head', ('inter', 'intra')), parts along dimension 0, may hold values from -6 to 6
- outputs: bfloat16 [32, 1024, 128], P('head', ('inter', 'intra')), parts along dimension 0, may hold values from -6 to 6
- out_grad: bfloat16 [32, 1024, 128], P('head', ('inter', 'intra')), parts along dimension 0, may hold values from -6 to 6
- log_norm: float32 [32, 1024], P('head', ('inter', 'intra')), parts along dimension 0, may hold values from 4 to 9
- key_values: bfloat16 [1024, 512], P(('inter', 'intra'), 'head'), parts along dimension 1, may hold values from -6 to 6
- key_exponent: int32 [128], P(('head', 'inter', 'intra')), parts along dimension 0, may hold values from -1 to 0
- value_values: bfloat16 [1024, 512], P(('inter', 'intra'), 'head'), parts along dimension 1, may hold values from -6 to 6
- value_exponent: int32 [128], P(('head', 'inter', 'intra')), parts along dimension 0, may hold values from -2 to 1
- span_order: int32 [64], P('head'), parts along dimension 0, may hold values from 0 to 15, each once
Outputs:
- query_grad: bfloat16 [32, 1024, 128], P('head', ('inter', 'intra')), parts along dimension 0
- key_grad: bfloat16 [1024, 512], P(('inter', 'intra'), 'head'), parts along dimension 1
- value_grad: bfloat16 [1024, 512], P(('inter', 'intra'), 'head'), parts along dimension 1
The draws below stay inside these ranges and needn't reach their ends.
There are 4 independent parts, one for each index of `head`. The reference program is written for one: setup_inputs(seed, part) draws one part's arguments, and reference() takes and returns one part's arrays. A program takes and returns all parts, laid end to end along the dimension named above; each array names one. Nothing has to cross between parts.
Inputs may be any that keep to these rules, and one draw needn't show every extreme that they name: `span_order`: a permutation of 0 to 15.
All inputs are finite; a program needn't handle non-finite values.
Results may differ from the reference program's by a relative error of at most 0.0049.
Values may be sent and summed in bfloat16 or wider, within the bound.
No kernel may reach another device: no remote copies, remote signals or barrier semaphores. Data moves between devices by JAX's collectives and lax.ppermute only.
A program may use at most 64 MiB of HBM per device.

```python
import math
import jax
import jax.numpy as jnp
from jax import lax

H = 8
HD = 128
TOK_DEV = 128
BLK = 32
TOKENS = 1024
SPANS = 16


def place_ends(result, key, low, high):
    longest = result.shape.index(max(result.shape))
    spots = []
    for shift in (0, 1):
        where = [jax.random.randint(jax.random.fold_in(key, axis), (), 0, length) for axis, length in enumerate(result.shape)]
        where[longest] = (where[longest] + shift) % result.shape[longest]
        spots.append(tuple(where))
    return result.at[spots[0]].set(low).at[spots[1]].set(high)


def shard_levels(key, dims, split, smallest, top_value):
    def one(dim, shards_of):
        heights = jax.random.uniform(jax.random.fold_in(jax.random.fold_in(key, 6), dim), (shards_of,), jnp.float32, smallest / len(split), top_value / len(split))
        return jnp.repeat(jnp.exp(heights), dims[dim] // shards_of).reshape((-1,) + (1,) * (len(dims) - dim - 1))

    level = one(*split[0])
    for cut in split[1:]:
        level = level * one(*cut)
    return level


def normal_values(rng, dims, spread, most, cuts=(), held_as=jnp.bfloat16):
    result = jax.random.normal(rng, dims, jnp.float32) * spread
    if len(cuts) > 0:
        result = shard_levels(rng, dims, cuts, -0.22, 0.18) * result
    return jnp.clip(result, min=-most, max=most).astype(held_as)


def setup_inputs(seed: int = 0, part: int = 0) -> dict:
    key_of = jax.random.split(jax.random.key(seed), 10)
    own_keys = jax.random.split(jax.random.fold_in(key_of[9], part), 10)
    return {
        "queries": normal_values(own_keys[0], (H, TOKENS, HD), 1.0, 6.0, ((1, 8),)),
        "outputs": normal_values(own_keys[1], (H, TOKENS, HD), 1.0, 6.0, ((1, 8),)),
        "out_grad": normal_values(own_keys[2], (H, TOKENS, HD), 1.0, 6.0, ((1, 8),)),
        "log_norm": jnp.clip(4.0 + 5.0 * jax.random.uniform(own_keys[3], (H, TOKENS), jnp.float32) ** shard_levels(own_keys[3], (H, TOKENS), ((1, 8),), -0.2, 0.2), 4.0, 9.0),
        "key_values": normal_values(own_keys[4], (TOKENS, HD), 1.0, 6.0, ((0, 8),)),
        "key_exponent": place_ends(jax.random.randint(own_keys[5], (TOKENS // BLK,), -1, 1), jax.random.fold_in(own_keys[5], 1), -1, 0).astype(jnp.int32),
        "value_values": normal_values(own_keys[6], (TOKENS, HD), 1.0, 6.0, ((0, 8),)),
        "value_exponent": place_ends(jax.random.randint(own_keys[7], (TOKENS // BLK,), -2, 2), jax.random.fold_in(own_keys[7], 1), -2, 1).astype(jnp.int32),
        "span_order": jax.random.permutation(own_keys[8], SPANS).astype(jnp.int32),
    }


def dequantize(stored, exponent):
    factor = jnp.exp2(jnp.repeat(exponent, BLK).astype(jnp.float32))
    return (stored.astype(jnp.float32) * factor[:, None]).astype(jnp.bfloat16)


def reference(queries, outputs, out_grad, log_norm, key_values, key_exponent, value_values, value_exponent, span_order):
    half = TOK_DEV // 2
    scale = HD ** -0.5
    keys = dequantize(key_values, key_exponent)
    values = dequantize(value_values, value_exponent)
    ids = jnp.arange(TOKENS, dtype=jnp.int32)
    position = span_order[ids // half] * half + ids % half
    query32 = queries.astype(jnp.float32)
    grad32 = out_grad.astype(jnp.float32)
    delta = jnp.sum(grad32 * outputs.astype(jnp.float32), -1)
    step_rows = math.gcd(TOKENS, 512)

    def advance(index, carry):
        query_acc, key_acc, value_acc = carry
        start = (index * step_rows).astype(jnp.int32)
        kblock = lax.dynamic_slice_in_dim(keys, start, step_rows, 0).astype(jnp.float32)
        vblock = lax.dynamic_slice_in_dim(values, start, step_rows, 0).astype(jnp.float32)
        kpos = lax.dynamic_slice_in_dim(position, start, step_rows, 0)
        scores = jnp.einsum('htd,kd->htk', query32, kblock) * scale
        live = kpos[None, None, :] <= position[None, :, None]
        probs = jnp.where(live, jnp.exp(scores - log_norm[:, :, None]), 0.0)
        probs_low = lax.optimization_barrier(probs.astype(jnp.bfloat16)).astype(jnp.float32)
        value_block = jnp.einsum('htk,htd->kd', probs_low, grad32)
        dprob = jnp.einsum('htd,kd->htk', grad32, vblock)
        dscore = lax.optimization_barrier((probs * (dprob - delta[:, :, None])).astype(jnp.bfloat16)).astype(jnp.float32)
        query_acc = query_acc + jnp.einsum('htk,kd->htd', dscore, kblock)
        key_block = jnp.einsum('htk,htd->kd', dscore, query32) * scale
        key_acc = lax.dynamic_update_slice_in_dim(key_acc, key_block, start, 0)
        value_acc = lax.dynamic_update_slice_in_dim(value_acc, value_block, start, 0)
        return query_acc, key_acc, value_acc

    init = (jnp.zeros((H, TOKENS, HD), jnp.float32), jnp.zeros((TOKENS, HD), jnp.float32), jnp.zeros((TOKENS, HD), jnp.float32))
    query_acc, key_acc, value_acc = lax.fori_loop(0, TOKENS // step_rows, advance, init)
    return (query_acc * scale).astype(jnp.bfloat16), key_acc.astype(jnp.bfloat16), value_acc.astype(jnp.bfloat16)
```

```python
import functools

import jax
import jax.numpy as jnp
from jax import lax
from jax.experimental import pallas as pl
from jax.experimental.pallas import tpu as pltpu
from jax.sharding import PartitionSpec as P


F32 = jnp.float32
BF16 = jnp.bfloat16
VMEM = pl.BlockSpec(memory_space=pltpu.VMEM)
SMEM = pl.BlockSpec(memory_space=pltpu.SMEM)
ROWS_BY_ROWS = (((1,), (1,)), ((), ()))
PLAIN = (((1,), (0,)), ((), ()))
COLS_BY_COLS = (((0,), (0,)), ((), ()))


def dot(a, b, dims):
    return lax.dot_general(a, b, dims, preferred_element_type=F32)


def prepare_kernel(
    key_exp, value_exp, keys, values, out_grad, outputs, log_norm, pack, stats
):
    rows, width = keys.shape
    heads = out_grad.shape[0]
    blocks = key_exp.shape[0]
    block = lax.broadcasted_iota(jnp.int32, (rows, 1), 0) // (rows // blocks)
    for stored, exps, at in ((keys, key_exp, 0), (values, value_exp, width)):
        exponent = jnp.zeros((rows, 1), jnp.int32)
        for b in range(blocks):
            exponent = jnp.where(block == b, exps[b], exponent)
        factor = lax.shift_left(jnp.ones_like(exponent), exponent + 2).astype(F32) * 0.25
        pack[:, at : at + width] = (stored[...].astype(F32) * factor).astype(BF16)
    stats[:heads] = log_norm[...]
    stats[heads:] = jnp.sum(out_grad[...].astype(F32) * outputs[...].astype(F32), -1)


def prepare(key_exp, value_exp, keys, values, out_grad, outputs, log_norm):
    rows, width = keys.shape
    heads = out_grad.shape[0]
    return pl.pallas_call(
        prepare_kernel,
        out_shape=(
            jax.ShapeDtypeStruct((rows, 2 * width), BF16),
            jax.ShapeDtypeStruct((2 * heads, rows), F32),
        ),
        in_specs=[SMEM, SMEM] + [VMEM] * 5,
        out_specs=(VMEM, VMEM),
        name="prepare",
    )(key_exp, value_exp, keys, values, out_grad, outputs, log_norm)


def attend_kernel(sides, shift, chunks, carried, last, order, queries, out_grad, stats, *refs):
    outer, inner = sides
    packs, refs = refs[:chunks], refs[chunks:]
    sums_in, refs = (refs[:chunks], refs[chunks:]) if carried else (None, refs)
    query_out, sums_out = refs[0], refs[1:]
    heads, rows, width = queries.shape
    half = rows // 2
    scale = width ** (-0.5)
    group = heads
    y, z = lax.axis_index("inter"), lax.axis_index("intra")

    def positions(device, ids):
        first, second = order[2 * device], order[2 * device + 1]
        return jnp.where(ids < half, first, second) * half + ids % half

    lanes = lax.broadcasted_iota(jnp.int32, (1, rows), 1)
    subs = lax.broadcasted_iota(jnp.int32, (rows, 1), 0)
    query_pos = positions(lax.rem(y + outer - shift, outer) * inner + z, lanes)
    live = jnp.concatenate(
        [
            positions(y * inner + lax.rem(z + inner - c, inner), subs) <= query_pos
            for c in range(chunks)
        ],
        0,
    )
    keys = jnp.concatenate([pack[:, :width] for pack in packs], 0)
    values = jnp.concatenate([pack[:, width:] for pack in packs], 0)
    key_sum = value_sum = None
    for g in range(0, heads, group):
        q = queries[g : g + group].reshape(group * rows, width)
        dout = out_grad[g : g + group].reshape(group * rows, width)
        scores = dot(keys, q, ROWS_BY_ROWS)
        dprob = dot(values, dout, ROWS_BY_ROWS)
        probs_low, dscore = [], []
        for j in range(group):
            at = slice(j * rows, (j + 1) * rows)
            log_norm = stats[g + j : g + j + 1, :]
            delta = stats[heads + g + j : heads + g + j + 1, :]
            probs = jnp.where(live, jnp.exp(scores[:, at] * scale - log_norm), 0.0)
            probs_low.append(probs.astype(BF16))
            dscore.append((probs * (dprob[:, at] - delta)).astype(BF16))
        probs_low = jnp.concatenate(probs_low, 1)
        dscore = jnp.concatenate(dscore, 1)
        value_part = dot(probs_low, dout, PLAIN)
        key_part = dot(dscore, q, PLAIN)
        value_sum = value_part if value_sum is None else value_sum + value_part
        key_sum = key_part if key_sum is None else key_sum + key_part
        query_part = dot(dscore, keys, COLS_BY_COLS).reshape(group, rows, width)
        query_out[g : g + group] = query_part.astype(query_out.dtype)
    for c in range(chunks):
        at = slice(c * rows, (c + 1) * rows)
        for total, lane in ((key_sum, 0), (value_sum, width)):
            piece = total[at]
            if carried:
                piece = piece + sums_in[c][:, lane : lane + width]
            sums_out[c][:, lane : lane + width] = piece.astype(sums_out[c].dtype)


def attend(sides, shift, last, order, queries, out_grad, stats, packs, sums):
    rows, width = queries.shape[1:]
    chunks = len(packs)
    carried = sums is not None
    sum_types = [BF16 if last and c > 0 else F32 for c in range(chunks)]
    inputs = [order, queries, out_grad, stats, *packs, *(sums or ())]
    query_sum, *sums = pl.pallas_call(
        functools.partial(attend_kernel, sides, shift, chunks, carried, last),
        out_shape=(
            jax.ShapeDtypeStruct(queries.shape, BF16 if shift else F32),
            *(jax.ShapeDtypeStruct((rows, 2 * width), t) for t in sum_types),
        ),
        in_specs=[SMEM] + [VMEM] * (len(inputs) - 1),
        out_specs=(VMEM,) * (1 + chunks),
        cost_estimate=pl.CostEstimate(
            flops=10 * queries.size * rows * chunks,
            bytes_accessed=8 * queries.size,
            transcendentals=queries.shape[0] * rows * rows * chunks,
        ),
        name=f"attend{shift}",
    )(*inputs)
    return query_sum, sums


def finish_kernel(parts, chunks, *refs):
    query_own, refs = refs[0], refs[1:]
    query_parts, refs = refs[:parts], refs[parts:]
    own, refs = refs[0], refs[1:]
    sum_parts, refs = refs[:chunks], refs[chunks:]
    query_grad, key_grad, value_grad = refs
    width = key_grad.shape[1]
    scale = width ** (-0.5)
    total = query_own[...]
    for part in query_parts:
        total = total + part[...].astype(F32)
    query_grad[...] = (total * scale).astype(BF16)
    total = own[...]
    for part in sum_parts:
        total = total + part[...].astype(F32)
    key_grad[...] = (total[:, :width] * scale).astype(BF16)
    value_grad[...] = total[:, width:].astype(BF16)


def finish(query_own, query_parts, own, sum_parts):
    rows, both = own.shape
    grad = jax.ShapeDtypeStruct((rows, both // 2), BF16)
    inputs = [query_own, *query_parts, own, *sum_parts]
    return pl.pallas_call(
        functools.partial(finish_kernel, len(query_parts), len(sum_parts)),
        out_shape=(jax.ShapeDtypeStruct(query_own.shape, BF16), grad, grad),
        in_specs=[VMEM] * len(inputs),
        out_specs=(VMEM,) * 3,
        name="finish",
    )(*inputs)


def move(x, axis, size, by):
    return lax.ppermute(x, axis, [(i, (i + by) % size) for i in range(size)])


def body(
    queries,
    outputs,
    out_grad,
    log_norm,
    key_values,
    key_exponent,
    value_values,
    value_exponent,
    span_order,
):
    outer = lax.axis_size("inter")
    inner = lax.axis_size("intra")
    sides = (outer, inner)
    far_queries = [move(queries, "inter", outer, j) for j in range(1, outer)]
    far_grads = [move(out_grad, "inter", outer, j) for j in range(1, outer)]
    pack, stats = prepare(
        key_exponent, value_exponent, key_values, value_values, out_grad, outputs, log_norm
    )
    far_stats = [move(stats, "inter", outer, j) for j in range(1, outer)]
    packs = [pack] + [move(pack, "intra", inner, c) for c in range(1, inner)]
    sets = list(
        zip([queries, *far_queries], [out_grad, *far_grads], [stats, *far_stats], strict=True)
    )
    sums, query_sums = None, []
    for j, (q, dout, stat) in enumerate(sets):
        query_sum, sums = attend(
            sides, j, j == len(sets) - 1, span_order, q, dout, stat, packs, sums
        )
        query_sums.append(query_sum)
    sum_parts = [move(sums[c], "intra", inner, -c) for c in range(1, inner)]
    query_parts = [move(query_sums[j], "inter", outer, -j) for j in range(1, outer)]
    return finish(query_sums[0], query_parts, sums[0], sum_parts)


def solution(mesh):
    return jax.shard_map(
        body,
        mesh=mesh,
        in_specs=(
            P("head", ("inter", "intra"), None),
            P("head", ("inter", "intra"), None),
            P("head", ("inter", "intra"), None),
            P("head", ("inter", "intra")),
            P(("inter", "intra"), "head"),
            P(("head", "inter", "intra")),
            P(("inter", "intra"), "head"),
            P(("head", "inter", "intra")),
            P("head"),
        ),
        out_specs=(
            P("head", ("inter", "intra"), None),
            P(("inter", "intra"), "head"),
            P(("inter", "intra"), "head"),
        ),
        check_vma=False,
    )
```

```python
import functools

import jax
import jax.numpy as jnp
from jax import lax
from jax.experimental import pallas as pl
from jax.experimental.pallas import tpu as pltpu
from jax.sharding import PartitionSpec as P


LIMIT = 24 << 20
LOG2E = 1.4426950408889634
F32 = jnp.float32
BF16 = jnp.bfloat16
VMEM = pl.BlockSpec(memory_space=pltpu.VMEM)
SMEM = pl.BlockSpec(memory_space=pltpu.SMEM)
HBM = pl.BlockSpec(memory_space=pltpu.HBM)
ROWS_BY_ROWS = (((1,), (1,)), ((), ()))
PLAIN = (((1,), (0,)), ((), ()))


def dot(a, b, dims):
    return lax.dot_general(a, b, dims, preferred_element_type=F32)


def in_hbm(*arrays):
    return [pltpu.with_memory_space_constraint(x, pltpu.HBM) for x in arrays]


def fetch(pairs, sems):
    copies = [pltpu.make_async_copy(a, b, sems.at[i]) for i, (a, b) in enumerate(pairs)]
    for copy in copies:
        copy.start()
    return [copy.wait for copy in copies]


def scale_kernel(keys, values, key_exp, value_exp, pack, stored, exps, sems):
    rows, width = keys.shape
    blocks = key_exp.shape[0]
    waits = fetch(
        (
            (key_exp, exps.at[0]),
            (value_exp, exps.at[1]),
            (keys, stored.at[0]),
            (values, stored.at[1]),
        ),
        sems,
    )
    for wait in waits:
        wait()
    block = lax.broadcasted_iota(jnp.int32, (rows, 1), 0) // (rows // blocks)
    for i in range(2):
        exponent = jnp.zeros((rows, 1), jnp.int32)
        for b in range(blocks):
            exponent = jnp.where(block == b, exps[i, b], exponent)
        factor = lax.shift_left(jnp.ones_like(exponent), exponent + 2).astype(F32) * 0.25
        pack[:, i * width : (i + 1) * width] = (stored[i].astype(F32) * factor).astype(BF16)


def scaled(keys, values, key_exp, value_exp):
    rows, width = keys.shape
    return pl.pallas_call(
        scale_kernel,
        out_shape=jax.ShapeDtypeStruct((rows, 2 * width), BF16),
        in_specs=[HBM] * 4,
        out_specs=VMEM,
        scratch_shapes=[
            pltpu.VMEM((2, rows, width), BF16),
            pltpu.SMEM((2, *key_exp.shape), jnp.int32),
            pltpu.SemaphoreType.DMA((4,)),
        ],
        compiler_params=pltpu.CompilerParams(vmem_limit_bytes=LIMIT),
        name="scaled",
    )(*in_hbm(keys, values, key_exp, value_exp))


def stats_kernel(out_grad, outputs, log_norm, stats, grads, outs, sems):
    heads = out_grad.shape[0]
    waits = fetch(((log_norm, stats.at[:heads]), (out_grad, grads), (outputs, outs)), sems)
    for wait in waits:
        wait()
    stats[heads:] = jnp.sum(grads[...].astype(F32) * outs[...].astype(F32), -1)


def row_stats(out_grad, outputs, log_norm):
    heads, rows, _ = out_grad.shape
    return pl.pallas_call(
        stats_kernel,
        out_shape=jax.ShapeDtypeStruct((2 * heads, rows), F32),
        in_specs=[HBM] * 3,
        out_specs=VMEM,
        scratch_shapes=[
            pltpu.VMEM(out_grad.shape, BF16),
            pltpu.VMEM(out_grad.shape, BF16),
            pltpu.SemaphoreType.DMA((3,)),
        ],
        compiler_params=pltpu.CompilerParams(vmem_limit_bytes=LIMIT),
        name="row_stats",
    )(*in_hbm(out_grad, outputs, log_norm))


def attend_kernel(sides, query_side, key_side, sources, counts, wants, carried, order, *refs):
    outer, inner = sides
    chunks, arrays = len(sources), counts[0]
    (queries, out_grad, stats), refs = refs[:3], refs[3:]
    packs, refs = refs[:arrays], refs[arrays:]
    extra, refs = (refs[0], refs[1:]) if counts[1] else (None, refs)
    query_in, refs = (refs[0], refs[1:]) if carried[0] else (None, refs)
    sums_in, refs = (refs[:chunks], refs[chunks:]) if carried[1] else (None, refs)
    query_out, sums_out = (refs[0], refs[1:]) if wants[0] else (None, refs)
    if counts[1]:
        together = refs[-1]
        for i, pack in enumerate((extra, *packs)):
            size = pack.shape[0]
            together[i * size : (i + 1) * size] = pack[...]
    heads, rows, width = queries.shape
    half = rows // 2
    scale = width ** (-0.5)
    y, z = lax.axis_index("inter"), lax.axis_index("intra")

    def device(side, place):
        return lax.rem(y + outer - side, outer) * inner + place

    def positions(index, ids):
        first, second = order[2 * index], order[2 * index + 1]
        return jnp.where(ids < half, first, second) * half + ids % half

    def joined(parts, axis):
        return parts[0] if len(parts) == 1 else jnp.concatenate(parts, axis)

    lanes = lax.broadcasted_iota(jnp.int32, (1, rows), 1)
    subs = lax.broadcasted_iota(jnp.int32, (rows, 1), 0)
    query_pos = positions(device(query_side, z), lanes)
    live = joined(
        [positions(device(key_side, back(z, c, inner)), subs) <= query_pos for c in sources], 0
    )
    keys = joined([pack[:, :width] for pack in packs], 0)
    values = joined([pack[:, width:] for pack in packs], 0)
    q = queries[...].reshape(heads * rows, width)
    dout = out_grad[...].reshape(heads * rows, width)
    scores = dot(keys, q, ROWS_BY_ROWS)
    dprob = dot(values, dout, ROWS_BY_ROWS)
    probs_low, dscore = [], []
    for j in range(heads):
        at = slice(j * rows, (j + 1) * rows)
        log_norm = stats[j : j + 1, :] * LOG2E
        delta = stats[heads + j : heads + j + 1, :]
        probs = jnp.where(live, jnp.exp2(scores[:, at] * (scale * LOG2E) - log_norm), 0.0)
        if wants[1]:
            probs_low.append(probs.astype(BF16))
        dscore.append((probs * (dprob[:, at] - delta)).astype(BF16))
    dscore = joined(dscore, 1)
    if wants[1]:
        value_sum = dot(joined(probs_low, 1), dout, PLAIN)
        key_sum = dot(dscore, q, PLAIN)
        for c in range(chunks):
            at = slice(c * rows, (c + 1) * rows)
            for total, lane in ((key_sum, 0), (value_sum, width)):
                piece = total[at]
                if carried[1]:
                    piece = piece + sums_in[c][:, lane : lane + width]
                sums_out[c][:, lane : lane + width] = piece.astype(sums_out[c].dtype)
    if wants[0]:
        query_sum = jnp.transpose(dot(jnp.transpose(keys), dscore, PLAIN))
        query_sum = query_sum.reshape(heads, rows, width)
        if carried[0]:
            query_sum = query_sum + query_in[...]
        if query_out.dtype == BF16:
            query_sum = query_sum * scale
        query_out[...] = query_sum.astype(query_out.dtype)


def attend(sides, places, order, side, packs, query_type, sum_types, query_in, sums_in, extra=None):
    queries, out_grad, stats = side
    rows, width = queries.shape[1:]
    steps = [c for key in packs for c in (key if isinstance(key, tuple) else (key,))]
    chunks = len(steps)
    counts = (len(packs), extra is not None)
    wants = (query_type is not None, sum_types is not None)
    carried = (query_in is not None, sums_in is not None)
    inputs = [order, queries, out_grad, stats, *packs.values()]
    inputs += [extra] if counts[1] else []
    inputs += ([query_in] if carried[0] else []) + (list(sums_in) if carried[1] else [])
    shapes = [jax.ShapeDtypeStruct(queries.shape, query_type)] if wants[0] else []
    if wants[1]:
        shapes += [jax.ShapeDtypeStruct((rows, 2 * width), t) for t in sum_types]
    if counts[1]:
        shapes.append(jax.ShapeDtypeStruct(((chunks + 1) * rows, 2 * width), BF16))
    outs = pl.pallas_call(
        functools.partial(
            attend_kernel, sides, *places, tuple(steps), counts, wants, carried
        ),
        out_shape=tuple(shapes),
        in_specs=[SMEM] + [VMEM] * (len(inputs) - 1),
        out_specs=(VMEM,) * len(shapes),
        cost_estimate=pl.CostEstimate(
            flops=10 * queries.size * rows * chunks,
            bytes_accessed=8 * queries.size,
            transcendentals=queries.shape[0] * rows * rows * chunks,
        ),
        compiler_params=pltpu.CompilerParams(vmem_limit_bytes=LIMIT),
    )(*inputs)
    return (outs[0] if wants[0] else None), list(outs[wants[0] :])


def finish_keys_kernel(own, *refs):
    parts, (_, key_grad, value_grad) = refs[:-3], refs[-3:]
    width = key_grad.shape[1]
    total = own[...]
    for part in parts:
        total = total + part[...].astype(F32)
    key_grad[...] = (total[:, :width] * width ** (-0.5)).astype(BF16)
    value_grad[...] = total[:, width:].astype(BF16)


def finish_keys(own, parts, after):
    rows, both = own.shape
    grad = jax.ShapeDtypeStruct((rows, both // 2), BF16)
    return pl.pallas_call(
        finish_keys_kernel,
        out_shape=(grad, grad),
        in_specs=[VMEM] * (1 + len(parts)) + [HBM],
        out_specs=(VMEM, VMEM),
        compiler_params=pltpu.CompilerParams(vmem_limit_bytes=LIMIT),
        name="finish_keys",
    )(own, *parts, *in_hbm(after))


def flips(size):
    return size & (size - 1) == 0


def back(place, step, size):
    return place ^ step if flips(size) else lax.rem(place + size - step, size)


def move_side(x, size, by):
    return lax.ppermute(x, "inter", [(i, (i + by) % size) for i in range(size)])


def move_place(x, size, step):
    if flips(size):
        return lax.ppermute(x, "intra", [(i, i ^ step) for i in range(size)])
    return lax.ppermute(x, "intra", [(i, (i + step) % size) for i in range(size)])


def steps(
    queries,
    outputs,
    out_grad,
    log_norm,
    key_values,
    key_exponent,
    value_values,
    value_exponent,
    span_order,
):
    outer = lax.axis_size("inter")
    inner = lax.axis_size("intra")
    far_queries = [move_side(queries, outer, j) for j in range(1, outer)]
    far_grads = [move_side(out_grad, outer, j) for j in range(1, outer)]
    pack = scaled(key_values, value_values, key_exponent, value_exponent)
    stats = row_stats(out_grad, outputs, log_norm)
    far_stats = [move_side(stats, outer, j) for j in range(1, outer)]
    rest = range(1, inner)
    own = {0: pack}
    row = {c: move_place(pack, inner, c) for c in rest}
    sides = [(queries, out_grad, stats), *zip(far_queries, far_grads, far_stats, strict=True)]
    shape = (outer, inner)
    query_own, sums = attend(shape, (0, 0), span_order, sides[0], own, F32, [F32], None, None)
    types = [F32] * len(rest)
    query_own, (*row_sums, together) = attend(
        shape, (0, 0), span_order, sides[0], row, F32, types, query_own, None, pack
    )
    sums = sums + row_sums
    all_steps = (0, *rest)
    far_packs = [{all_steps: move_side(together, outer, j)} for j in range(1, outer)]
    for j in range(1, outer):
        types = [F32] + [BF16 if j == outer - 1 else F32] * len(rest)
        _, sums = attend(shape, (j, 0), span_order, sides[j], own | row, None, types, None, sums)
    sum_parts = [move_place(sums[c], inner, c if flips(inner) else -c) for c in rest]
    for j in range(1, outer):
        last = BF16 if j == outer - 1 else F32
        query_own, _ = attend(
            shape, (0, j), span_order, sides[0], far_packs[j - 1], last, None, query_own, None
        )
    return (query_own, *finish_keys(sums[0], sum_parts, query_own))


def solution(mesh):
    return jax.shard_map(
        steps,
        mesh=mesh,
        in_specs=(
            P("head", ("inter", "intra"), None),
            P("head", ("inter", "intra"), None),
            P("head", ("inter", "intra"), None),
            P("head", ("inter", "intra")),
            P(("inter", "intra"), "head"),
            P(("head", "inter", "intra")),
            P(("inter", "intra"), "head"),
            P(("head", "inter", "intra")),
            P("head"),
        ),
        out_specs=(
            P("head", ("inter", "intra"), None),
            P(("inter", "intra"), "head"),
            P(("inter", "intra"), "head"),
        ),
        check_vma=False,
    )
```
